512 devices in a mesh: wide: 64 (over z, y_hi, core), narrow: 8 (over x, y_lo).
Axes of the slice: x: 4, y: 8 (y_hi: 4, y_lo: 2; y = y_hi * 2 + y_lo), z: 8, core: 2. Of those that a mesh axis runs over, the one named last changes fastest.
Arguments:
- hidden_in: bfloat16 [16384, 2048], P('wide', 'narrow'), may hold values from -64 to 64
- cache_lengths: int32 [128], P('wide'), may hold values from 1 to 1023, as said below
- cache_offsets: int32 [128], P('wide'), may hold values from 0 to 65535, as said below
- cache_kv: bfloat16 [2, 2, 65536, 2048], P(None, None, 'wide', 'narrow'), may hold values from -16 to 16
- w_qkv: bfloat16 [2048, 3, 2048], P('wide', None, 'narrow'), may hold values from -0.125 to 0.125
- qkv_bias: bfloat16 [3, 2048], P(None, 'narrow'), may hold values from -40 to 40
- w_out: bfloat16 [2048, 2048], P('wide', 'narrow'), may hold values from -0.125 to 0.125
- out_bias: bfloat16 [2048], P('narrow'), may hold values from -3 to 3
- norm_gain: bfloat16 [2048], P('narrow'), may hold values from 0.2 to 5
- norm_shift: bfloat16 [2048], P('narrow'), may hold values from -3 to 3
Outputs:
- hidden_out: bfloat16 [16384, 2048], P('wide', 'narrow')
- new_cache: bfloat16 [2, 2, 16384, 2048], P(None, None, 'wide', 'narrow')
The draws below stay inside these ranges and needn't reach their ends.
Inputs may be any that keep to these rules, and one draw needn't show every extreme that they name: `cache_lengths`: the cached lengths of the 2 requests r with the same r // 2 sum to at most 1024; for some such group exactly 1024, and in it one request has 1023 rows. Request r's cache is rows cache_offsets[r] to cache_offsets[r] + cache_lengths[r] - 1 of the packed cache, all within rows (r // 2) * 1024 to (r // 2 + 1) * 1024 - 1; the row ranges of different requests are disjoint.
All inputs are finite; a program needn't handle non-finite values.
Results may differ from the reference program's by a relative error of at most 0.02.
Values may be sent and summed in bfloat16 or wider, within the bound.
No kernel may reach another device: no remote copies, remote signals or barrier semaphores. Data moves between devices by JAX's collectives and lax.ppermute only.
A program may use at most 64 MiB of HBM per device.

```python
import math
import jax
import jax.numpy as jnp
from jax import lax

HEADS = 16
HEAD = 128
D = 2048
SPAN = 128
REQ_DEV = 2
CACHE_DEV = 1024
LAYERS = 2
REQUESTS = 128
TOKENS = 16384
CACHE_ROWS = 65536


def layout_helper(key):
    base = jax.random.fold_in(key, 4242)
    keys = jax.random.split(base, 6)
    groups = REQUESTS // REQ_DEV
    shifts = jax.random.randint(keys[0], (groups,), 0, 4)
    capacity = jnp.right_shift(jnp.full((groups,), CACHE_DEV, jnp.int32), shifts)
    reduction = jax.random.randint(keys[1], (groups,), 0, 1 << 20) % (capacity // 4 + 1)
    totals = jnp.maximum(capacity - reduction, REQ_DEV)
    chosen = jax.random.randint(keys[2], (), 0, groups)
    is_chosen = jnp.arange(groups) == chosen
    totals = jnp.where(is_chosen, CACHE_DEV, totals).astype(jnp.int32)
    shares = jax.random.randint(keys[3], (groups, REQ_DEV), 1, 65536)
    lengths = 1 + (totals - REQ_DEV)[:, None] * shares // jnp.sum(shares, axis=1, keepdims=True)
    lengths = lengths.at[:, -1].set(totals - jnp.sum(lengths[:, :-1], axis=1))
    heavy = jnp.where(jnp.arange(REQ_DEV) == REQ_DEV - 1, CACHE_DEV - REQ_DEV + 1, 1).astype(lengths.dtype)
    lengths = jnp.where(is_chosen[:, None], heavy[None, :], lengths)
    ranking = jax.random.randint(keys[4], (groups, REQ_DEV), 0, 1 << 20) * REQ_DEV + jnp.arange(REQ_DEV)[None, :]
    order = jnp.argsort(ranking, axis=1)
    stored_lengths = jnp.take_along_axis(lengths, order, axis=1)
    leading_gap = jax.random.randint(keys[5], (groups,), 0, 1 << 20) % (CACHE_DEV - totals + 1)
    stored_starts = leading_gap[:, None] + jnp.cumsum(stored_lengths, axis=1) - stored_lengths
    inverse = jnp.argsort(order, axis=1)
    starts = jnp.take_along_axis(stored_starts, inverse, axis=1) + (jnp.arange(groups) * CACHE_DEV)[:, None]
    return (lengths.reshape(-1).astype(jnp.int32), starts.reshape(-1).astype(jnp.int32))


def draw_cache_lengths(key, part):
    lengths, starts = layout_helper(key)
    return lengths


def draw_cache_offsets(key, part):
    lengths, starts = layout_helper(key)
    return starts


def draw_hidden_in(key, part):
    keys = jax.random.split(jax.random.fold_in(key, 3), 3)
    position = jnp.arange(D, dtype=jnp.float32) / (D - 1)
    column_scale = jnp.exp(math.log(0.3) + math.log(10.0) * position) * jax.random.uniform(keys[0], (D,), jnp.float32, 0.7, 1.4)
    row_scale = jnp.exp(jax.random.uniform(keys[1], (TOKENS, 1), jnp.float32, math.log(0.3), math.log(3.0)))
    noise = jnp.clip(jax.random.normal(keys[2], (TOKENS, D), jnp.float32), -4.0, 4.0)
    return (noise * column_scale[None, :] * row_scale).astype(jnp.bfloat16)


def draw_cache_kv(key, part):
    shape = (LAYERS, 2, CACHE_ROWS, D)
    noise_key = jax.random.fold_in(key, 5)
    values = jnp.clip(jax.random.normal(noise_key, shape, jnp.float32), -6.0, 6.0)
    return values.astype(jnp.bfloat16)


def draw_qkv_bias(key, part):
    values = 0.5 * jnp.clip(jax.random.normal(jax.random.fold_in(key, 1), (3, D), jnp.float32), -6.0, 6.0)
    return values.astype(jnp.bfloat16)


def draw_norm_gain(key, part):
    position = jnp.arange(D, dtype=jnp.float32) / (D - 1)
    rising = jnp.exp(math.log(0.5) + math.log(6.0) * position)
    jitter = jax.random.uniform(jax.random.fold_in(key, 2), (D,), jnp.float32, 0.75, 1.33)
    return (rising * jitter).astype(jnp.bfloat16)


def block_levels(stream_key, dims, pieces, smallest, largest):
    factor_of = 1.0
    for dim, parts in pieces:
        steps = jax.random.uniform(jax.random.fold_in(jax.random.fold_in(stream_key, 6), dim), (parts,), jnp.float32, smallest / len(pieces), largest / len(pieces))
        factor_of = factor_of * jnp.repeat(jnp.exp(steps), dims[dim] // parts).reshape((-1,) + (1,) * (len(dims) - 1 - dim))
    return factor_of


def bell_draw(own_key, shape, deviation, reach, cuts=(), held_as=jnp.bfloat16):
    values = deviation * jax.random.normal(own_key, shape, jnp.float32)
    if cuts:
        values = values * block_levels(own_key, shape, cuts, -0.22, 0.18)
    return jnp.clip(values, -reach, reach).astype(held_as)


def setup_inputs(seed: int = 0) -> dict:
    key_of = jax.random.split(jax.random.key(seed), 11)
    return {
        "hidden_in": draw_hidden_in(jax.random.fold_in(key_of[10], 71), 0),
        "cache_lengths": draw_cache_lengths(jax.random.fold_in(key_of[10], 71), 0),
        "cache_offsets": draw_cache_offsets(jax.random.fold_in(key_of[10], 71), 0),
        "cache_kv": draw_cache_kv(jax.random.fold_in(key_of[10], 71), 0),
        "w_qkv": bell_draw(key_of[4], (D, 3, D), D ** -0.5, 0.125, ((0, 64), (2, 8))),
        "qkv_bias": draw_qkv_bias(jax.random.fold_in(key_of[10], 71), 0),
        "w_out": bell_draw(key_of[6], (D, D), D ** -0.5, 0.125, ((0, 64), (1, 8))),
        "out_bias": bell_draw(key_of[7], (D,), 0.5, 3.0, ((0, 8),)),
        "norm_gain": draw_norm_gain(jax.random.fold_in(key_of[10], 71), 0),
        "norm_shift": bell_draw(key_of[9], (D,), 0.5, 3.0, ((0, 8),)),
    }


EPSILON = 1e-05
NEGATIVE = -1e+30

def normalize(summed, norm_gain, norm_shift):
    values = summed.astype(jnp.float32)
    row_means = lax.optimization_barrier(jnp.mean(values, axis=1, keepdims=True))
    centered = values - row_means
    row_spread = lax.optimization_barrier(jnp.mean(centered * centered, axis=1, keepdims=True))
    scaled = centered * lax.rsqrt(row_spread + EPSILON)
    return (scaled * norm_gain.astype(jnp.float32) + norm_shift.astype(jnp.float32)).astype(jnp.bfloat16)

def reference(hidden_in, cache_lengths, cache_offsets, cache_kv, w_qkv, qkv_bias, w_out, out_bias, norm_gain, norm_shift):
    scale_factor = 1.0 / HEAD ** 0.5
    qkv_flat = w_qkv.reshape(D, 3 * D)
    bias_flat = qkv_bias.astype(jnp.float32).reshape(3 * D)
    causal = jnp.arange(SPAN)[:, None] >= jnp.arange(SPAN)[None, :]
    layer_input = hidden_in
    appended = []
    for layer_index in range(LAYERS):
        projections = jnp.dot(layer_input, qkv_flat, preferred_element_type=jnp.float32) + bias_flat
        queries = projections[:, :D].astype(jnp.bfloat16)
        keys_new = projections[:, D:2 * D].astype(jnp.bfloat16)
        values_new = projections[:, 2 * D:].astype(jnp.bfloat16)
        appended.append(jnp.stack([keys_new, values_new]))
        cache_keys = cache_kv[layer_index, 0]
        cache_values = cache_kv[layer_index, 1]

        def attend_one(request):
            block_start = (request // REQ_DEV * CACHE_DEV).astype(jnp.int32)
            token_start = (request * SPAN).astype(jnp.int32)
            keys_block = lax.dynamic_slice_in_dim(cache_keys, block_start, CACHE_DEV, 0).reshape(CACHE_DEV, HEADS, HEAD)
            values_block = lax.dynamic_slice_in_dim(cache_values, block_start, CACHE_DEV, 0).reshape(CACHE_DEV, HEADS, HEAD)
            query_rows = lax.dynamic_slice_in_dim(queries, token_start, SPAN, 0).reshape(SPAN, HEADS, HEAD)
            keys_fresh = lax.dynamic_slice_in_dim(keys_new, token_start, SPAN, 0).reshape(SPAN, HEADS, HEAD)
            values_fresh = lax.dynamic_slice_in_dim(values_new, token_start, SPAN, 0).reshape(SPAN, HEADS, HEAD)
            rows_global = block_start + jnp.arange(CACHE_DEV, dtype=jnp.int32)
            row_start = cache_offsets[request]
            row_stop = row_start + cache_lengths[request]
            live_rows = (rows_global >= row_start) & (rows_global < row_stop)
            mask_all = jnp.concatenate([jnp.broadcast_to(live_rows[None, :], (SPAN, CACHE_DEV)), causal], axis=1)
            keys_all = jnp.concatenate([keys_block, keys_fresh], axis=0).astype(jnp.float32)
            values_all = jnp.concatenate([values_block, values_fresh], axis=0).astype(jnp.float32)
            scores = jnp.einsum('qhd,khd->hqk', query_rows.astype(jnp.float32), keys_all) * scale_factor
            masked = jnp.where(mask_all[None], scores, NEGATIVE)
            top_score = lax.optimization_barrier(jnp.max(masked, axis=2, keepdims=True))
            weights = jnp.where(mask_all[None], jnp.exp(masked - top_score), 0.0)
            probabilities = (weights / lax.optimization_barrier(jnp.sum(weights, axis=2, keepdims=True))).astype(jnp.bfloat16)
            combined = jnp.einsum('hqk,khd->qhd', probabilities.astype(jnp.float32), values_all)
            return combined.astype(jnp.bfloat16).reshape(SPAN, D)
        attended = lax.map(attend_one, jnp.arange(REQUESTS, dtype=jnp.int32)).reshape(TOKENS, D)
        projected = jnp.dot(attended, w_out, preferred_element_type=jnp.float32) + out_bias.astype(jnp.float32)
        summed = (projected + layer_input.astype(jnp.float32)).astype(jnp.bfloat16)
        layer_input = normalize(summed, norm_gain, norm_shift)
    return (layer_input, jnp.stack(appended))
```

```python
import functools
import math

import jax
import jax.numpy as jnp
from jax import lax
from jax.experimental import pallas as pl
from jax.experimental.pallas import tpu as pltpu
from jax.sharding import Mesh
from jax.sharding import PartitionSpec as P

HEAD = 128
SPAN = 128
EPSILON = 1e-05
NEGATIVE = -1e30
AXES = ("z", "yh", "c", "x", "yl")
SIZES = (8, 4, 2, 4, 2)
WIDE = ("z", "yh", "c")
NARROW = ("x", "yl")
SWAP = [(0, 1), (1, 0)]
VMEM_LIMIT = 40 * 1024 * 1024
F32 = jnp.float32
BF16 = jnp.bfloat16


def spread(x, axes, count):
    return lax.all_to_all(jnp.broadcast_to(x[None], (count,) + x.shape), axes, 0, 0, tiled=True)


def dot(a, b):
    return jnp.dot(a, b, preferred_element_type=F32)


def dot_t(a, b):
    return lax.dot_general(a, b, (((1,), (1,)), ((), ())), preferred_element_type=F32)


def rows_of(own, other, low, z, j):
    parts = []
    for y in range(4):
        mine, theirs = own[z, y, j], other[z, y, j]
        parts += [jnp.where(low, mine, theirs), jnp.where(low, theirs, mine)]
    return jnp.concatenate(parts, axis=0)


def attention_kernel(
    first, info, starts, stops, x_ref, gs_ref, bias_ref, cache, prev, own, other, *rest
):
    if first:
        att_ref, new_ref = rest
        x = x_ref
    else:
        att_ref, new_ref, res_ref, x = rest
        total = jnp.zeros((256, 1), F32)
        for n in range(8):
            total += jnp.sum(x_ref[n, 0:256, :].astype(F32), axis=1, keepdims=True)
        mean = total / 2048.0
        spread_sum = jnp.zeros((256, 1), F32)
        for n in range(8):
            centered = x_ref[n, 0:256, :].astype(F32) - mean
            spread_sum += jnp.sum(centered * centered, axis=1, keepdims=True)
        scale = lax.rsqrt(spread_sum / 2048.0 + EPSILON)
        for n in range(8):
            both = gs_ref[n].astype(F32)
            gain = both[0:1]
            shift = both[1:2]
            x[n] = ((x_ref[n, 0:256, :].astype(F32) - mean) * scale * gain + shift).astype(BF16)
        res_ref[...] = x[info[1]]
    low = info[0] == 0
    bias = bias_ref[...]
    parts = []
    for j in range(3):
        acc = dot(x[0, 0:256, :], rows_of(own, other, low, 0, j))
        for n in range(1, 8):
            acc += dot(x[n, 0:256, :], rows_of(own, other, low, n, j))
        parts.append((acc + bias[j : j + 1]).astype(BF16))
    q, k_new, v_new = parts
    new_ref[0, 0] = k_new
    new_ref[0, 1] = v_new
    factor = 1.0 / math.sqrt(HEAD)
    column = lax.broadcasted_iota(jnp.int32, (1, 1024), 1)
    causal = lax.broadcasted_iota(jnp.int32, (SPAN, SPAN), 0) >= lax.broadcasted_iota(
        jnp.int32, (SPAN, SPAN), 1
    )
    for r in range(2):
        rows = slice(r * SPAN, (r + 1) * SPAN)
        live = (column >= starts[r]) & (column < stops[r])
        for h in range(2):
            cols = slice(h * HEAD, (h + 1) * HEAD)
            qh = q[rows, cols]
            sc = jnp.where(live, dot_t(qh, cache[0, 0, :, cols]) * factor, NEGATIVE)
            sn = jnp.where(causal, dot_t(qh, k_new[rows, cols]) * factor, NEGATIVE)
            top = jnp.maximum(
                jnp.max(sc, axis=1, keepdims=True), jnp.max(sn, axis=1, keepdims=True)
            )
            pc = jnp.exp(sc - top)
            pn = jnp.exp(sn - top)
            norm = jnp.sum(pc, axis=1, keepdims=True) + jnp.sum(pn, axis=1, keepdims=True)
            out = dot(pc.astype(BF16), cache[0, 1, :, cols]) + dot(
                pn.astype(BF16), v_new[rows, cols]
            )
            att_ref[rows, cols] = (out / norm).astype(BF16)


def piece_specs(j, count):
    return [pl.BlockSpec((8, 4, count, 32, 256), lambda i: (0, 0, j, 0, 0))] * 2


def attention(first, layer, info, starts, stops, x, gathered, bias, cache, prev, pieces):
    smem = pl.BlockSpec(memory_space=pltpu.SMEM)

    def whole(a):
        return pl.BlockSpec(a.shape, lambda i: (0,) * a.ndim)

    rows = x.shape[1]
    in_specs = [
        smem,
        smem,
        smem,
        pl.BlockSpec((8, rows, 256), lambda i: (0, 0, 0)),
        pl.BlockSpec((8, 16, 256), lambda i: (0, 0 if first else 16, 0)),
        whole(bias),
        pl.BlockSpec((1, 2, 1024, 256), lambda i: (layer, 0, 0, 0)),
        pl.BlockSpec(memory_space=pl.ANY),
    ] + piece_specs(0, 3)
    tile = jax.ShapeDtypeStruct((256, 256), BF16)
    out_shape = [tile, jax.ShapeDtypeStruct((2, 2, 256, 256), BF16)]
    tile_spec = pl.BlockSpec((256, 256), lambda i: (0, 0))
    out_specs = [tile_spec, pl.BlockSpec((1, 2, 256, 256), lambda i: (layer, 0, 0, 0))]
    scratch = []
    aliases = {}
    if not first:
        out_shape.append(tile)
        out_specs.append(tile_spec)
        scratch.append(pltpu.VMEM((8, 256, 256), BF16))
        aliases = {7: 1}
    return pl.pallas_call(
        functools.partial(attention_kernel, first),
        grid=(1,),
        out_shape=out_shape,
        in_specs=in_specs,
        out_specs=out_specs,
        scratch_shapes=scratch,
        input_output_aliases=aliases,
        compiler_params=pltpu.CompilerParams(vmem_limit_bytes=VMEM_LIMIT),
        cost_estimate=pl.CostEstimate(
            flops=2 * 256 * 2048 * 768 + 4 * 256 * 1152 * 256,
            bytes_accessed=6 << 20,
            transcendentals=256 * 1152 * 2,
        ),
        name="attention",
    )(info, starts, stops, x, gathered, bias, cache, prev, *pieces)


def project_kernel(last, info, att, bias_ref, res_ref, gs_ref, own, other, *rest):
    out_ref = rest[0]
    low = info[0] == 0
    acc = dot(att[0], rows_of(own, other, low, 0, 0))
    for n in range(1, 8):
        acc += dot(att[n], rows_of(own, other, low, n, 0))
    summed = (acc + bias_ref[0:1, :] + res_ref[...].astype(F32)).astype(BF16)
    out_ref[0:256, :] = summed
    if last:
        values = summed.astype(F32)
        mean = jnp.sum(values, axis=1, keepdims=True) / 256.0
        centered = values - mean
        spread_sum = jnp.sum(centered * centered, axis=1, keepdims=True)
        lane = lax.broadcasted_iota(jnp.int32, (256, 128), 1)
        stats = jnp.where(lane == 0, mean, spread_sum)
        rest[1][...] = stats.T[0:8, :]
    else:
        out_ref[256:272, :] = gs_ref[...]


def project(last, info, att, bias, res, gs, pieces):
    def whole(a):
        return pl.BlockSpec(a.shape, lambda i: (0,) * a.ndim)

    out_shape = [jax.ShapeDtypeStruct((256 if last else 272, 256), BF16)]
    if last:
        out_shape.append(jax.ShapeDtypeStruct((8, 256), F32))
    return pl.pallas_call(
        functools.partial(project_kernel, last),
        grid=(1,),
        out_shape=out_shape,
        in_specs=[pl.BlockSpec(memory_space=pltpu.SMEM)]
        + [whole(a) for a in (att, bias, res, gs)]
        + piece_specs(3, 1),
        out_specs=[whole(a) for a in out_shape],
        compiler_params=pltpu.CompilerParams(vmem_limit_bytes=VMEM_LIMIT),
        cost_estimate=pl.CostEstimate(
            flops=2 * 256 * 2048 * 256, bytes_accessed=3 << 20, transcendentals=0
        ),
        name="project",
    )(info, att, bias, res, gs, *pieces)


def finish_kernel(stats, summed, gain_ref, shift_ref, out_ref):
    means = [stats[n, 0:1, :] for n in range(8)]
    mean = functools.reduce(lambda a, b: a + b, means) / 8.0
    total = jnp.zeros((1, 256), F32)
    for n in range(8):
        offset = means[n] - mean
        total += stats[n, 1:2, :] + 256.0 * offset * offset
    scale = lax.rsqrt(total / 2048.0 + EPSILON)
    row = lax.broadcasted_iota(jnp.int32, (128, 256), 0)
    columns = jnp.where(row == 0, mean, scale).T
    values = summed[...].astype(F32)
    scaled = (values - columns[:, 0:1]) * columns[:, 1:2]
    out_ref[...] = (scaled * gain_ref[...].astype(F32) + shift_ref[...].astype(F32)).astype(BF16)


def finish(stats, summed, gain, shift):
    return pl.pallas_call(
        finish_kernel,
        out_shape=jax.ShapeDtypeStruct((256, 256), BF16),
        name="finish",
    )(stats, summed, gain, shift)


def shards(
    hidden_in,
    cache_lengths,
    cache_offsets,
    cache_kv,
    w_qkv,
    qkv_bias,
    w_out,
    out_bias,
    norm_gain,
    norm_shift,
):
    cache_count = cache_kv.shape[2]
    info = jnp.stack([lax.axis_index("c"), lax.axis_index(NARROW), lax.axis_index("yh")])
    starts = cache_offsets - lax.axis_index(WIDE) * cache_count
    stops = starts + cache_lengths
    gs = jnp.concatenate([norm_gain[None], norm_shift[None], jnp.zeros((14, 256), BF16)], axis=0)
    bias = jnp.pad(qkv_bias.astype(F32), ((0, 5), (0, 0)))
    out_b = jnp.broadcast_to(out_bias.astype(F32)[None], (8, 256))
    gain = norm_gain.reshape(1, -1)
    shift = norm_shift.reshape(1, -1)

    pieces = jnp.concatenate([w_qkv.transpose(1, 0, 2), w_out[None]], axis=0)
    near = spread(pieces, "yh", 4)
    near, entry = lax.optimization_barrier((near, hidden_in))
    own = lax.all_gather(near.reshape(512, 256), "z", axis=0, tiled=True)
    gathered = spread(entry, NARROW, 8)
    own, gathered = lax.optimization_barrier((own, gathered))
    other = lax.ppermute(own, "c", SWAP)
    pieces = [own.reshape(8, 4, 4, 32, 256), other.reshape(8, 4, 4, 32, 256)]

    blank = jnp.zeros((8, 128), BF16)
    att, new_cache = attention(
        True, 0, info, starts, stops, gathered, gathered, bias, cache_kv, blank, pieces
    )
    heads = spread(att, NARROW, 8)
    (summed,) = project(False, info, heads, out_b, hidden_in, gs, pieces)
    rows = spread(summed, NARROW, 8)
    att, new_cache, carried = attention(
        False, 1, info, starts, stops, rows, rows, bias, cache_kv, new_cache, pieces
    )
    heads = spread(att, NARROW, 8)
    summed, stats = project(True, info, heads, out_b, carried, gs, pieces)
    hidden_out = finish(spread(stats, NARROW, 8), summed, gain, shift)
    return hidden_out, new_cache


def solution(mesh):
    split = Mesh(mesh.devices.reshape(SIZES), AXES)
    in_specs = (
        P(WIDE, NARROW),
        P(WIDE),
        P(WIDE),
        P(None, None, WIDE, NARROW),
        P(WIDE, None, NARROW),
        P(None, NARROW),
        P(WIDE, NARROW),
        P(NARROW),
        P(NARROW),
        P(NARROW),
    )
    out_specs = (P(WIDE, NARROW), P(None, None, WIDE, NARROW))
    return jax.shard_map(shards, mesh=split, in_specs=in_specs, out_specs=out_specs, check_vma=False)
```

```python
import functools
import math

import jax
import jax.numpy as jnp
from jax import lax
from jax.experimental import pallas as pl
from jax.experimental.pallas import tpu as pltpu
from jax.sharding import Mesh
from jax.sharding import PartitionSpec as P

HEAD = 128
SPAN = 128
EPSILON = 1e-05
NEGATIVE = -1e30
AXES = ("zh", "zl", "yh", "c", "x", "yl")
SIZES = (4, 2, 4, 2, 4, 2)
WIDE = ("zh", "zl", "yh", "c")
NARROW = ("x", "yl")
SWAP = [(0, 1), (1, 0)]
VMEM_LIMIT = 16 * 1024 * 1024
F32 = jnp.float32
BF16 = jnp.bfloat16


def spread(x, axes, count):
    return lax.all_to_all(jnp.broadcast_to(x[None], (count,) + x.shape), axes, 0, 0, tiled=True)


def dot(a, b):
    return jnp.dot(a, b, preferred_element_type=F32)


def dot_t(a, b):
    return lax.dot_general(a, b, (((1,), (1,)), ((), ())), preferred_element_type=F32)


def rows_of(pieces, info, z, j):
    same, same_swap, away, away_swap = pieces
    zh, zl = z // 2, z % 2
    low = info[0] == 0
    here = info[1] == zl
    parts = []
    for y in range(4):
        mine = jnp.where(here, same[zh, y, j], away[zh, y, j])
        theirs = jnp.where(here, same_swap[zh, y, j], away_swap[zh, y, j])
        parts += [jnp.where(low, mine, theirs), jnp.where(low, theirs, mine)]
    return jnp.concatenate(parts, axis=0)


def attention_kernel(layer, info, starts, stops, params, cache_ref, prev, *rest):
    pieces, rest = rest[:4], rest[4:]
    count = 4 if layer == 0 else 2
    inputs, rest = rest[:count], rest[count:]
    att_ref, new_ref, extra_ref, new, cache, sems, x = rest
    fetch = pltpu.make_async_copy(cache_ref.at[layer], cache, sems.at[2])
    fetch.start()
    if layer == 0:
        for k in range(8):
            source = info[2] ^ k
            x[source] = inputs[k // 2][k % 2, 0:256, :]
            extra_ref[source] = inputs[k // 2][k % 2, 256:272, :]
    else:
        x_ref, gs_ref = inputs
        total = jnp.zeros((256, 1), F32)
        for n in range(8):
            total += jnp.sum(x_ref[n].astype(F32), axis=1, keepdims=True)
        mean = total / 2048.0
        spread_sum = jnp.zeros((256, 1), F32)
        for n in range(8):
            centered = x_ref[n].astype(F32) - mean
            spread_sum += jnp.sum(centered * centered, axis=1, keepdims=True)
        scale = lax.rsqrt(spread_sum / 2048.0 + EPSILON)
        for n in range(8):
            both = gs_ref[n].astype(F32)
            normed = (x_ref[n].astype(F32) - mean) * scale * both[0:1] + both[1:2]
            x[n] = normed.astype(BF16)
        extra_ref[...] = x[info[2]]
    bias = params[...]
    parts = []
    copies = []
    for j in range(3):
        acc = dot(x[0], rows_of(pieces, info, 0, j))
        for n in range(1, 8):
            acc += dot(x[n], rows_of(pieces, info, n, j))
        parts.append((acc + bias[j : j + 1]).astype(BF16))
        if j > 0:
            new[j - 1] = parts[j]
            copy = pltpu.make_async_copy(new.at[j - 1], new_ref.at[layer, j - 1], sems.at[j - 1])
            copy.start()
            copies.append(copy)
    q, k_new, v_new = parts
    fetch.wait()
    factor = 1.0 / math.sqrt(HEAD)
    column = lax.broadcasted_iota(jnp.int32, (1, 1024), 1)
    causal = lax.broadcasted_iota(jnp.int32, (SPAN, SPAN), 0) >= lax.broadcasted_iota(
        jnp.int32, (SPAN, SPAN), 1
    )
    for r in range(2):
        rows = slice(r * SPAN, (r + 1) * SPAN)
        live = (column >= starts[r]) & (column < stops[r])
        for h in range(2):
            cols = slice(h * HEAD, (h + 1) * HEAD)
            qh = q[rows, cols]
            sc = jnp.where(live, dot_t(qh, cache[0, :, cols]) * factor, NEGATIVE)
            sn = jnp.where(causal, dot_t(qh, k_new[rows, cols]) * factor, NEGATIVE)
            top = jnp.maximum(
                jnp.max(sc, axis=1, keepdims=True), jnp.max(sn, axis=1, keepdims=True)
            )
            pc = jnp.exp(sc - top)
            pn = jnp.exp(sn - top)
            norm = jnp.sum(pc, axis=1, keepdims=True) + jnp.sum(pn, axis=1, keepdims=True)
            out = dot(pc.astype(BF16), cache[1, :, cols]) + dot(
                pn.astype(BF16), v_new[rows, cols]
            )
            att_ref[rows, cols] = (out / norm).astype(BF16)
    for copy in copies:
        copy.wait()


def attention(layer, info, starts, stops, params, cache, prev, pieces, inputs):
    smem = pl.BlockSpec(memory_space=pltpu.SMEM)
    vmem = pl.BlockSpec(memory_space=pltpu.VMEM)
    anywhere = pl.BlockSpec(memory_space=pl.ANY)
    tile = jax.ShapeDtypeStruct((256, 256), BF16)
    vectors = jax.ShapeDtypeStruct((8, 16, 256), BF16)
    out_shape = [
        tile,
        jax.ShapeDtypeStruct((2, 2, 256, 256), BF16),
        vectors if layer == 0 else tile,
    ]
    return pl.pallas_call(
        functools.partial(attention_kernel, layer),
        out_shape=out_shape,
        in_specs=[smem] * 3 + [vmem, anywhere, anywhere] + [vmem] * (4 + len(inputs)),
        out_specs=[vmem, anywhere, vmem],
        scratch_shapes=[
            pltpu.VMEM((2, 256, 256), BF16),
            pltpu.VMEM((2, 1024, 256), BF16),
            pltpu.SemaphoreType.DMA((3,)),
            pltpu.VMEM((8, 256, 256), BF16),
        ],
        input_output_aliases={5: 1} if layer > 0 else {},
        compiler_params=pltpu.CompilerParams(vmem_limit_bytes=VMEM_LIMIT),
        cost_estimate=pl.CostEstimate(
            flops=2 * 256 * 2048 * 768 + 4 * 256 * 1152 * 256,
            bytes_accessed=6 << 20,
            transcendentals=256 * 1152 * 2,
        ),
        name="attention",
    )(info, starts, stops, params, cache, prev, *pieces, *inputs)


def project_kernel(last, info, att, params, res_ref, *rest):
    pieces, out_ref = rest[:4], rest[4]
    acc = dot(att[0], rows_of(pieces, info, 0, 3))
    for n in range(1, 8):
        acc += dot(att[n], rows_of(pieces, info, n, 3))
    bias = params[...]
    summed = (acc + bias[3:4] + res_ref[...].astype(F32)).astype(BF16)
    out_ref[...] = summed
    if last:
        values = summed.astype(F32)
        mean = jnp.sum(values, axis=1, keepdims=True) / 256.0
        centered = values - mean
        spread_sum = jnp.sum(centered * centered, axis=1, keepdims=True)
        lane = lax.broadcasted_iota(jnp.int32, (256, 128), 1)
        stats = jnp.where(lane == 0, mean, spread_sum)
        rest[5][...] = stats.T[0:8, :]


def project(last, info, att, params, res, pieces):
    vmem = pl.BlockSpec(memory_space=pltpu.VMEM)
    out_shape = [jax.ShapeDtypeStruct((256, 256), BF16)]
    if last:
        out_shape.append(jax.ShapeDtypeStruct((8, 256), F32))
    return pl.pallas_call(
        functools.partial(project_kernel, last),
        out_shape=out_shape,
        in_specs=[pl.BlockSpec(memory_space=pltpu.SMEM)] + [vmem] * 7,
        out_specs=[vmem] * len(out_shape),
        compiler_params=pltpu.CompilerParams(vmem_limit_bytes=VMEM_LIMIT),
        cost_estimate=pl.CostEstimate(
            flops=2 * 256 * 2048 * 256, bytes_accessed=3 << 20, transcendentals=0
        ),
        name="project",
    )(info, att, params, res, *pieces)


def finish_kernel(stats, summed, params, out_ref):
    means = [stats[n, 0:1, :] for n in range(8)]
    mean = functools.reduce(lambda a, b: a + b, means) / 8.0
    total = jnp.zeros((1, 256), F32)
    for n in range(8):
        offset = means[n] - mean
        total += stats[n, 1:2, :] + 256.0 * offset * offset
    scale = lax.rsqrt(total / 2048.0 + EPSILON)
    row = lax.broadcasted_iota(jnp.int32, (128, 256), 0)
    columns = jnp.where(row == 0, mean, scale).T
    values = summed[...].astype(F32)
    scaled = (values - columns[:, 0:1]) * columns[:, 1:2]
    gains = params[...]
    out_ref[...] = (scaled * gains[4:5] + gains[5:6]).astype(BF16)


def finish(stats, summed, params):
    vmem = pl.BlockSpec(memory_space=pltpu.VMEM)
    return pl.pallas_call(
        finish_kernel,
        out_shape=jax.ShapeDtypeStruct((256, 256), BF16),
        in_specs=[vmem] * 3,
        out_specs=vmem,
        compiler_params=pltpu.CompilerParams(vmem_limit_bytes=VMEM_LIMIT),
        name="finish",
    )(stats, summed, params)


def shards(
    hidden_in,
    cache_lengths,
    cache_offsets,
    cache_kv,
    w_qkv,
    qkv_bias,
    w_out,
    out_bias,
    norm_gain,
    norm_shift,
):
    cache_count = cache_kv.shape[2]
    info = jnp.stack([lax.axis_index("c"), lax.axis_index("zl"), lax.axis_index(NARROW)])
    starts = cache_offsets - lax.axis_index(WIDE) * cache_count
    stops = starts + cache_lengths
    vectors = [qkv_bias, out_bias[None], norm_gain[None], norm_shift[None]]
    params = jnp.pad(jnp.concatenate(vectors, axis=0).astype(F32), ((0, 2), (0, 0)))
    payload = jnp.concatenate(
        [hidden_in, norm_gain[None], norm_shift[None], jnp.zeros((14, 256), BF16)], axis=0
    )

    pieces = jnp.concatenate([w_qkv.transpose(1, 0, 2), w_out[None]], axis=0)
    near = spread(pieces, "yh", 4)
    near, payload = lax.optimization_barrier((near, payload))
    same = spread(near, "zh", 4)
    blocks = jnp.stack([payload, lax.ppermute(payload, "yl", SWAP)])
    blocks = [blocks] + [
        lax.ppermute(blocks, "x", [(i, i ^ k) for i in range(4)]) for k in range(1, 4)
    ]
    same, blocks, params, info, starts, stops = lax.optimization_barrier(
        (same, blocks, params, info, starts, stops)
    )
    left = lax.ppermute(same[:2], ("zh", "zl"), [(i, (i + 1) % 8) for i in range(8)])
    right = lax.ppermute(same[2:], ("zh", "zl"), [(i, (i - 1) % 8) for i in range(8)])
    same_swap = lax.ppermute(same, "c", SWAP)
    away = jnp.concatenate([left, right], axis=0)
    pieces = [same, same_swap, away, lax.ppermute(away, "c", SWAP)]

    blank = jnp.zeros((8, 128), BF16)
    att, new_cache, vectors = attention(
        0, info, starts, stops, params, cache_kv, blank, pieces, blocks
    )
    heads = spread(att, NARROW, 8)
    (summed,) = project(False, info, heads, params, hidden_in, pieces)
    rows = spread(summed, NARROW, 8)
    att, new_cache, carried = attention(
        1, info, starts, stops, params, cache_kv, new_cache, pieces, [rows, vectors]
    )
    heads = spread(att, NARROW, 8)
    summed, stats = project(True, info, heads, params, carried, pieces)
    hidden_out = finish(spread(stats, NARROW, 8), summed, params)
    return hidden_out, new_cache


def solution(mesh):
    split = Mesh(mesh.devices.reshape(SIZES), AXES)
    in_specs = (
        P(WIDE, NARROW),
        P(WIDE),
        P(WIDE),
        P(None, None, WIDE, NARROW),
        P(WIDE, None, NARROW),
        P(None, NARROW),
        P(WIDE, NARROW),
        P(NARROW),
        P(NARROW),
        P(NARROW),
    )
    out_specs = (P(WIDE, NARROW), P(None, None, WIDE, NARROW))
    return jax.shard_map(shards, mesh=split, in_specs=in_specs, out_specs=out_specs, check_vma=False)
```

```python
import functools
import math

import jax
import jax.numpy as jnp
from jax import lax
from jax.experimental import pallas as pl
from jax.experimental.pallas import tpu as pltpu
from jax.sharding import Mesh
from jax.sharding import PartitionSpec as P

HEAD = 128
SPAN = 128
EPSILON = 1e-05
NEGATIVE = -1e30
AXES = ("zh", "zl", "yh", "c", "x", "yl")
SIZES = (4, 2, 4, 2, 4, 2)
WIDE = ("zh", "zl", "yh", "c")
NARROW = ("x", "yl")
SWAP = [(0, 1), (1, 0)]
VMEM_LIMIT = 16 * 1024 * 1024
F32 = jnp.float32
BF16 = jnp.bfloat16


def spread(x, axes, count):
    return lax.all_to_all(jnp.broadcast_to(x[None], (count,) + x.shape), axes, 0, 0, tiled=True)


def dot(a, b):
    return jnp.dot(a, b, preferred_element_type=F32)


def dot_t(a, b):
    return lax.dot_general(a, b, (((1,), (1,)), ((), ())), preferred_element_type=F32)


def rows_of(pieces, info, z, j):
    same, same_swap, away, away_swap = pieces
    zh, zl = z // 2, z % 2
    low = info[0] == 0
    here = info[1] == zl
    parts = []
    for y in range(4):
        mine = jnp.where(here, same[zh, y, j], away[zh, y, j])
        theirs = jnp.where(here, same_swap[zh, y, j], away_swap[zh, y, j])
        parts += [jnp.where(low, mine, theirs), jnp.where(low, theirs, mine)]
    return jnp.concatenate(parts, axis=0)


def attention_kernel(layer, info, starts, stops, params, cache_ref, prev, *rest):
    pieces, rest = rest[:4], rest[4:]
    count = 2 if layer == 0 else 3
    inputs, rest = rest[:count], rest[count:]
    att_ref, new_ref = rest[:2]
    new, cache, sems, x = rest[-4:]
    fetch = pltpu.make_async_copy(cache_ref.at[layer], cache, sems.at[2])
    fetch.start()
    if layer == 0:
        for k in range(8):
            x[info[2] ^ k] = inputs[k % 2][k // 2, 0:256, :]
    else:
        x_ref = inputs[0]
        total = jnp.zeros((256, 1), F32)
        for n in range(8):
            total += jnp.sum(x_ref[n].astype(F32), axis=1, keepdims=True)
        mean = total / 2048.0
        spread_sum = jnp.zeros((256, 1), F32)
        for n in range(8):
            centered = x_ref[n].astype(F32) - mean
            spread_sum += jnp.sum(centered * centered, axis=1, keepdims=True)
        scale = lax.rsqrt(spread_sum / 2048.0 + EPSILON)
        for k in range(8):
            source = info[2] ^ k
            both = inputs[1 + k % 2][k // 2, 256:272, :].astype(F32)
            normed = (x_ref[source].astype(F32) - mean) * scale * both[0:1] + both[1:2]
            x[source] = normed.astype(BF16)
        rest[2][...] = x[info[2]]
    bias = params[...]
    parts = []
    copies = []
    for j in range(3):
        acc = dot(x[0], rows_of(pieces, info, 0, j))
        for n in range(1, 8):
            acc += dot(x[n], rows_of(pieces, info, n, j))
        parts.append((acc + bias[j : j + 1]).astype(BF16))
        if j > 0:
            new[j - 1] = parts[j]
            copy = pltpu.make_async_copy(new.at[j - 1], new_ref.at[layer, j - 1], sems.at[j - 1])
            copy.start()
            copies.append(copy)
    q, k_new, v_new = parts
    fetch.wait()
    factor = math.log2(math.e) / math.sqrt(HEAD)
    column = lax.broadcasted_iota(jnp.int32, (1, 1024), 1)
    causal = lax.broadcasted_iota(jnp.int32, (SPAN, SPAN), 0) >= lax.broadcasted_iota(
        jnp.int32, (SPAN, SPAN), 1
    )
    for r in range(2):
        rows = slice(r * SPAN, (r + 1) * SPAN)
        live = (column >= starts[r]) & (column < stops[r])
        for h in range(2):
            cols = slice(h * HEAD, (h + 1) * HEAD)
            qh = q[rows, cols]
            sc = jnp.where(live, dot_t(qh, cache[0, :, cols]) * factor, NEGATIVE)
            sn = jnp.where(causal, dot_t(qh, k_new[rows, cols]) * factor, NEGATIVE)
            top = jnp.maximum(
                jnp.max(sc, axis=1, keepdims=True), jnp.max(sn, axis=1, keepdims=True)
            )
            pc = jnp.exp2(sc - top)
            pn = jnp.exp2(sn - top)
            norm = jnp.sum(pc, axis=1, keepdims=True) + jnp.sum(pn, axis=1, keepdims=True)
            out = dot(pc.astype(BF16), cache[1, :, cols]) + dot(
                pn.astype(BF16), v_new[rows, cols]
            )
            att_ref[rows, cols] = (out / norm).astype(BF16)
    for copy in copies:
        copy.wait()


def attention(layer, info, starts, stops, params, cache, prev, pieces, inputs):
    smem = pl.BlockSpec(memory_space=pltpu.SMEM)
    vmem = pl.BlockSpec(memory_space=pltpu.VMEM)
    anywhere = pl.BlockSpec(memory_space=pl.ANY)
    tile = jax.ShapeDtypeStruct((256, 256), BF16)
    out_shape = [tile, jax.ShapeDtypeStruct((2, 2, 256, 256), BF16)]
    out_specs = [vmem, anywhere]
    if layer > 0:
        out_shape.append(tile)
        out_specs.append(vmem)
    return pl.pallas_call(
        functools.partial(attention_kernel, layer),
        out_shape=out_shape,
        in_specs=[smem] * 3 + [vmem, anywhere, anywhere] + [vmem] * (4 + len(inputs)),
        out_specs=out_specs,
        scratch_shapes=[
            pltpu.VMEM((2, 256, 256), BF16),
            pltpu.VMEM((2, 1024, 256), BF16),
            pltpu.SemaphoreType.DMA((3,)),
            pltpu.VMEM((8, 256, 256), BF16),
        ],
        input_output_aliases={5: 1} if layer > 0 else {},
        compiler_params=pltpu.CompilerParams(vmem_limit_bytes=VMEM_LIMIT),
        cost_estimate=pl.CostEstimate(
            flops=2 * 256 * 2048 * 768 + 4 * 256 * 1152 * 256,
            bytes_accessed=6 << 20,
            transcendentals=256 * 1152 * 2,
        ),
        name="attention",
    )(info, starts, stops, params, cache, prev, *pieces, *inputs)


def project_kernel(last, info, att, params, res_ref, *rest):
    pieces, out_ref = rest[:4], rest[4]
    acc = dot(att[0], rows_of(pieces, info, 0, 3))
    for n in range(1, 8):
        acc += dot(att[n], rows_of(pieces, info, n, 3))
    bias = params[...]
    summed = (acc + bias[3:4] + res_ref[...].astype(F32)).astype(BF16)
    out_ref[...] = summed
    if last:
        values = summed.astype(F32)
        mean = jnp.sum(values, axis=1, keepdims=True) / 256.0
        centered = values - mean
        spread_sum = jnp.sum(centered * centered, axis=1, keepdims=True)
        lane = lax.broadcasted_iota(jnp.int32, (256, 128), 1)
        stats = jnp.where(lane == 0, mean, spread_sum)
        rest[5][...] = stats.T[0:8, :]


def project(last, info, att, params, res, pieces):
    vmem = pl.BlockSpec(memory_space=pltpu.VMEM)
    out_shape = [jax.ShapeDtypeStruct((256, 256), BF16)]
    if last:
        out_shape.append(jax.ShapeDtypeStruct((8, 256), F32))
    return pl.pallas_call(
        functools.partial(project_kernel, last),
        out_shape=out_shape,
        in_specs=[pl.BlockSpec(memory_space=pltpu.SMEM)] + [vmem] * 7,
        out_specs=[vmem] * len(out_shape),
        compiler_params=pltpu.CompilerParams(vmem_limit_bytes=VMEM_LIMIT),
        cost_estimate=pl.CostEstimate(
            flops=2 * 256 * 2048 * 256, bytes_accessed=3 << 20, transcendentals=0
        ),
        name="project",
    )(info, att, params, res, *pieces)


def finish_kernel(stats, summed, params, out_ref):
    means = [stats[n, 0:1, :] for n in range(8)]
    mean = functools.reduce(lambda a, b: a + b, means) / 8.0
    total = jnp.zeros((1, 256), F32)
    for n in range(8):
        offset = means[n] - mean
        total += stats[n, 1:2, :] + 256.0 * offset * offset
    scale = lax.rsqrt(total / 2048.0 + EPSILON)
    row = lax.broadcasted_iota(jnp.int32, (128, 256), 0)
    columns = jnp.where(row == 0, mean, scale).T
    values = summed[...].astype(F32)
    scaled = (values - columns[:, 0:1]) * columns[:, 1:2]
    gains = params[...]
    out_ref[...] = (scaled * gains[4:5] + gains[5:6]).astype(BF16)


def finish(stats, summed, params):
    vmem = pl.BlockSpec(memory_space=pltpu.VMEM)
    return pl.pallas_call(
        finish_kernel,
        out_shape=jax.ShapeDtypeStruct((256, 256), BF16),
        in_specs=[vmem] * 3,
        out_specs=vmem,
        compiler_params=pltpu.CompilerParams(vmem_limit_bytes=VMEM_LIMIT),
        name="finish",
    )(stats, summed, params)


def shards(
    hidden_in,
    cache_lengths,
    cache_offsets,
    cache_kv,
    w_qkv,
    qkv_bias,
    w_out,
    out_bias,
    norm_gain,
    norm_shift,
):
    cache_count = cache_kv.shape[2]
    info = jnp.stack([lax.axis_index("c"), lax.axis_index("zl"), lax.axis_index(NARROW)])
    starts = cache_offsets - lax.axis_index(WIDE) * cache_count
    stops = starts + cache_lengths
    vectors = [qkv_bias, out_bias[None], norm_gain[None], norm_shift[None]]
    params = jnp.pad(jnp.concatenate(vectors, axis=0).astype(F32), ((0, 2), (0, 0)))

    pieces = jnp.concatenate([w_qkv.transpose(1, 0, 2), w_out[None]], axis=0)
    payload = jnp.concatenate(
        [hidden_in, norm_gain[None], norm_shift[None], jnp.zeros((14, 256), BF16)], axis=0
    )
    mine = jnp.stack(
        [payload]
        + [lax.ppermute(payload, "x", [(i, i ^ k) for i in range(4)]) for k in range(1, 4)]
    )
    same = spread(pieces, ("zh", "yh"), 16).reshape(4, 4, 4, 32, 256)
    same, mine, params, info, starts, stops = lax.optimization_barrier(
        (same, mine, params, info, starts, stops)
    )
    left = lax.ppermute(same[:2], ("zh", "zl"), [(i, (i + 1) % 8) for i in range(8)])
    right = lax.ppermute(same[2:], ("zh", "zl"), [(i, (i - 1) % 8) for i in range(8)])
    same_swap = lax.ppermute(same, "c", SWAP)
    blocks = [mine, lax.ppermute(mine, "yl", SWAP)]
    left, right, blocks = lax.optimization_barrier((left, right, blocks))
    away = jnp.concatenate([left, right], axis=0)
    pieces = [same, same_swap, away, lax.ppermute(away, "c", SWAP)]

    blank = jnp.zeros((8, 128), BF16)
    att, new_cache = attention(
        0, info, starts, stops, params, cache_kv, blank, pieces, blocks
    )
    heads = spread(att, NARROW, 8)
    (summed,) = project(False, info, heads, params, hidden_in, pieces)
    rows = spread(summed, NARROW, 8)
    att, new_cache, carried = attention(
        1, info, starts, stops, params, cache_kv, new_cache, pieces, [rows] + blocks
    )
    heads = spread(att, NARROW, 8)
    summed, stats = project(True, info, heads, params, carried, pieces)
    hidden_out = finish(spread(stats, NARROW, 8), summed, params)
    return hidden_out, new_cache


def solution(mesh):
    split = Mesh(mesh.devices.reshape(SIZES), AXES)
    in_specs = (
        P(WIDE, NARROW),
        P(WIDE),
        P(WIDE),
        P(None, None, WIDE, NARROW),
        P(WIDE, None, NARROW),
        P(None, NARROW),
        P(WIDE, NARROW),
        P(NARROW),
        P(NARROW),
        P(NARROW),
    )
    out_specs = (P(WIDE, NARROW), P(None, None, WIDE, NARROW))
    return jax.shard_map(shards, mesh=split, in_specs=in_specs, out_specs=out_specs, check_vma=False)
```

```python
import functools
import math

import jax
import jax.numpy as jnp
from jax import lax
from jax.experimental import pallas as pl
from jax.experimental.pallas import tpu as pltpu
from jax.sharding import Mesh
from jax.sharding import PartitionSpec as P

HEAD = 128
SPAN = 128
EPSILON = 1e-05
NEGATIVE = -1e30
AXES = ("zh", "zl", "yh", "c", "x", "yl")
SIZES = (4, 2, 4, 2, 4, 2)
WIDE = ("zh", "zl", "yh", "c")
NARROW = ("x", "yl")
SWAP = [(0, 1), (1, 0)]
VMEM_LIMIT = 16 * 1024 * 1024
F32 = jnp.float32
BF16 = jnp.bfloat16


def spread(x, axes, count):
    return lax.all_to_all(jnp.broadcast_to(x[None], (count,) + x.shape), axes, 0, 0, tiled=True)


def dot(a, b):
    return jnp.dot(a, b, preferred_element_type=F32)


def dot_t(a, b):
    return lax.dot_general(a, b, (((1,), (1,)), ((), ())), preferred_element_type=F32)


def rows_of(pieces, info, z, j):
    same, same_swap, away, away_swap = pieces
    zh, zl = z // 2, z % 2
    low = info[0] == 0
    here = info[1] == zl
    parts = []
    for y in range(4):
        mine = jnp.where(here, same[zh, y, j], away[zh, y, j])
        theirs = jnp.where(here, same_swap[zh, y, j], away_swap[zh, y, j])
        parts += [jnp.where(low, mine, theirs), jnp.where(low, theirs, mine)]
    return jnp.concatenate(parts, axis=0)


def attention_kernel(layer, info, starts, stops, params, cache_ref, prev, *rest):
    pieces, rest = rest[:4], rest[4:]
    count = 2 if layer == 0 else 3
    inputs, rest = rest[:count], rest[count:]
    att_ref, new_ref = rest[:2]
    new, cache, sems, x = rest[-4:]
    fetch = pltpu.make_async_copy(cache_ref.at[layer], cache, sems.at[2])
    fetch.start()
    if layer == 0:
        for k in range(8):
            x[info[2] ^ k] = inputs[k % 2][k // 2, 0:256, :]
    else:
        x_ref = inputs[0]
        total = jnp.zeros((256, 256), F32)
        for n in range(8):
            total += x_ref[n].astype(F32)
        mean = jnp.sum(total, axis=1, keepdims=True) / 2048.0
        squares = jnp.zeros((256, 256), F32)
        for n in range(8):
            centered = x_ref[n].astype(F32) - mean
            squares += centered * centered
        spread_sum = jnp.sum(squares, axis=1, keepdims=True)
        scale = lax.rsqrt(spread_sum / 2048.0 + EPSILON)
        for k in range(8):
            source = info[2] ^ k
            both = inputs[1 + k % 2][k // 2, 256:272, :].astype(F32)
            normed = (x_ref[source].astype(F32) - mean) * scale * both[0:1] + both[1:2]
            x[source] = normed.astype(BF16)
        rest[2][...] = x[info[2]]
    bias = params[...]
    parts = []
    copies = []
    for j in range(3):
        acc = dot(x[0], rows_of(pieces, info, 0, j))
        for n in range(1, 8):
            acc += dot(x[n], rows_of(pieces, info, n, j))
        parts.append((acc + bias[j : j + 1]).astype(BF16))
        if j > 0:
            new[j - 1] = parts[j]
            copy = pltpu.make_async_copy(new.at[j - 1], new_ref.at[layer, j - 1], sems.at[j - 1])
            copy.start()
            copies.append(copy)
    q, k_new, v_new = parts
    fetch.wait()
    factor = math.log2(math.e) / math.sqrt(HEAD)
    column = lax.broadcasted_iota(jnp.int32, (1, 1024), 1)
    causal = lax.broadcasted_iota(jnp.int32, (SPAN, SPAN), 0) >= lax.broadcasted_iota(
        jnp.int32, (SPAN, SPAN), 1
    )
    for r in range(2):
        rows = slice(r * SPAN, (r + 1) * SPAN)
        live = (column >= starts[r]) & (column < stops[r])
        for h in range(2):
            cols = slice(h * HEAD, (h + 1) * HEAD)
            qh = q[rows, cols]
            sc = jnp.where(live, dot_t(qh, cache[0, :, cols]) * factor, NEGATIVE)
            sn = jnp.where(causal, dot_t(qh, k_new[rows, cols]) * factor, NEGATIVE)
            top = jnp.maximum(
                jnp.max(sc, axis=1, keepdims=True), jnp.max(sn, axis=1, keepdims=True)
            )
            pc = jnp.exp2(sc - top)
            pn = jnp.exp2(sn - top)
            norm = jnp.sum(pc, axis=1, keepdims=True) + jnp.sum(pn, axis=1, keepdims=True)
            out = dot(pc.astype(BF16), cache[1, :, cols]) + dot(
                pn.astype(BF16), v_new[rows, cols]
            )
            att_ref[rows, cols] = (out / norm).astype(BF16)
    for copy in copies:
        copy.wait()


def attention(layer, info, starts, stops, params, cache, prev, pieces, inputs):
    smem = pl.BlockSpec(memory_space=pltpu.SMEM)
    vmem = pl.BlockSpec(memory_space=pltpu.VMEM)
    anywhere = pl.BlockSpec(memory_space=pl.ANY)
    tile = jax.ShapeDtypeStruct((256, 256), BF16)
    out_shape = [tile, jax.ShapeDtypeStruct((2, 2, 256, 256), BF16)]
    out_specs = [vmem, anywhere]
    if layer > 0:
        out_shape.append(tile)
        out_specs.append(vmem)
    return pl.pallas_call(
        functools.partial(attention_kernel, layer),
        out_shape=out_shape,
        in_specs=[smem] * 3 + [vmem, anywhere, anywhere] + [vmem] * (4 + len(inputs)),
        out_specs=out_specs,
        scratch_shapes=[
            pltpu.VMEM((2, 256, 256), BF16),
            pltpu.VMEM((2, 1024, 256), BF16),
            pltpu.SemaphoreType.DMA((3,)),
            pltpu.VMEM((8, 256, 256), BF16),
        ],
        input_output_aliases={5: 1} if layer > 0 else {},
        compiler_params=pltpu.CompilerParams(vmem_limit_bytes=VMEM_LIMIT),
        cost_estimate=pl.CostEstimate(
            flops=2 * 256 * 2048 * 768 + 4 * 256 * 1152 * 256,
            bytes_accessed=6 << 20,
            transcendentals=256 * 1152 * 2,
        ),
        name="attention",
    )(info, starts, stops, params, cache, prev, *pieces, *inputs)


def project_kernel(last, info, att, params, res_ref, *rest):
    pieces, out_ref = rest[:4], rest[4]
    acc = dot(att[0], rows_of(pieces, info, 0, 3))
    for n in range(1, 8):
        acc += dot(att[n], rows_of(pieces, info, n, 3))
    bias = params[...]
    summed = (acc + bias[3:4] + res_ref[...].astype(F32)).astype(BF16)
    out_ref[...] = summed
    if last:
        values = summed.astype(F32)
        mean = jnp.sum(values, axis=1, keepdims=True) / 256.0
        centered = values - mean
        spread_sum = jnp.sum(centered * centered, axis=1, keepdims=True)
        lane = lax.broadcasted_iota(jnp.int32, (256, 128), 1)
        stats = jnp.where(lane == 0, mean, spread_sum)
        rest[5][...] = stats.T[0:8, :]


def project(last, info, att, params, res, pieces):
    vmem = pl.BlockSpec(memory_space=pltpu.VMEM)
    out_shape = [jax.ShapeDtypeStruct((256, 256), BF16)]
    if last:
        out_shape.append(jax.ShapeDtypeStruct((8, 256), F32))
    return pl.pallas_call(
        functools.partial(project_kernel, last),
        out_shape=out_shape,
        in_specs=[pl.BlockSpec(memory_space=pltpu.SMEM)] + [vmem] * 7,
        out_specs=[vmem] * len(out_shape),
        compiler_params=pltpu.CompilerParams(vmem_limit_bytes=VMEM_LIMIT),
        cost_estimate=pl.CostEstimate(
            flops=2 * 256 * 2048 * 256, bytes_accessed=3 << 20, transcendentals=0
        ),
        name="project",
    )(info, att, params, res, *pieces)


def finish_kernel(stats, summed, params, out_ref):
    means = [stats[n, 0:1, :] for n in range(8)]
    mean = functools.reduce(lambda a, b: a + b, means) / 8.0
    total = jnp.zeros((1, 256), F32)
    for n in range(8):
        offset = means[n] - mean
        total += stats[n, 1:2, :] + 256.0 * offset * offset
    scale = lax.rsqrt(total / 2048.0 + EPSILON)
    row = lax.broadcasted_iota(jnp.int32, (128, 256), 0)
    columns = jnp.where(row == 0, mean, scale).T
    values = summed[...].astype(F32)
    scaled = (values - columns[:, 0:1]) * columns[:, 1:2]
    gains = params[...]
    out_ref[...] = (scaled * gains[4:5] + gains[5:6]).astype(BF16)


def finish(stats, summed, params):
    vmem = pl.BlockSpec(memory_space=pltpu.VMEM)
    return pl.pallas_call(
        finish_kernel,
        out_shape=jax.ShapeDtypeStruct((256, 256), BF16),
        in_specs=[vmem] * 3,
        out_specs=vmem,
        compiler_params=pltpu.CompilerParams(vmem_limit_bytes=VMEM_LIMIT),
        name="finish",
    )(stats, summed, params)


def shards(
    hidden_in,
    cache_lengths,
    cache_offsets,
    cache_kv,
    w_qkv,
    qkv_bias,
    w_out,
    out_bias,
    norm_gain,
    norm_shift,
):
    cache_count = cache_kv.shape[2]
    info = jnp.stack([lax.axis_index("c"), lax.axis_index("zl"), lax.axis_index(NARROW)])
    starts = cache_offsets - lax.axis_index(WIDE) * cache_count
    stops = starts + cache_lengths
    vectors = [qkv_bias, out_bias[None], norm_gain[None], norm_shift[None]]
    params = jnp.pad(jnp.concatenate(vectors, axis=0).astype(F32), ((0, 2), (0, 0)))

    pieces = jnp.concatenate([w_qkv.transpose(1, 0, 2), w_out[None]], axis=0)
    payload = jnp.concatenate(
        [hidden_in, norm_gain[None], norm_shift[None], jnp.zeros((14, 256), BF16)], axis=0
    )
    mine = jnp.stack(
        [payload]
        + [lax.ppermute(payload, "x", [(i, i ^ k) for i in range(4)]) for k in range(1, 4)]
    )
    same = spread(pieces, ("zh", "yh"), 16).reshape(4, 4, 4, 32, 256)
    same, mine, params, info, starts, stops = lax.optimization_barrier(
        (same, mine, params, info, starts, stops)
    )
    left = lax.ppermute(same[:2], ("zh", "zl"), [(i, (i + 1) % 8) for i in range(8)])
    right = lax.ppermute(same[2:], ("zh", "zl"), [(i, (i - 1) % 8) for i in range(8)])
    same_swap = lax.ppermute(same, "c", SWAP)
    blocks = [mine, lax.ppermute(mine, "yl", SWAP)]
    left, right, blocks = lax.optimization_barrier((left, right, blocks))
    away = jnp.concatenate([left, right], axis=0)
    pieces = [same, same_swap, away, lax.ppermute(away, "c", SWAP)]

    blank = jnp.zeros((8, 128), BF16)
    att, new_cache = attention(
        0, info, starts, stops, params, cache_kv, blank, pieces, blocks
    )
    heads = spread(att, NARROW, 8)
    (summed,) = project(False, info, heads, params, hidden_in, pieces)
    rows = spread(summed, NARROW, 8)
    att, new_cache, carried = attention(
        1, info, starts, stops, params, cache_kv, new_cache, pieces, [rows] + blocks
    )
    heads = spread(att, NARROW, 8)
    summed, stats = project(True, info, heads, params, carried, pieces)
    hidden_out = finish(spread(stats, NARROW, 8), summed, params)
    return hidden_out, new_cache


def solution(mesh):
    split = Mesh(mesh.devices.reshape(SIZES), AXES)
    in_specs = (
        P(WIDE, NARROW),
        P(WIDE),
        P(WIDE),
        P(None, None, WIDE, NARROW),
        P(WIDE, None, NARROW),
        P(None, NARROW),
        P(WIDE, NARROW),
        P(NARROW),
        P(NARROW),
        P(NARROW),
    )
    out_specs = (P(WIDE, NARROW), P(None, None, WIDE, NARROW))
    return jax.shard_map(shards, mesh=split, in_specs=in_specs, out_specs=out_specs, check_vma=False)
```
